32 devices in a mesh: groups: 2 (over x), rows: 16 (over z, y, core).
Axes of the slice: x: 2, y: 2, z: 4, core: 2. Of those that a mesh axis runs over, the one named last changes fastest.
Arguments:
- frames: bfloat16 [2048, 3, 256], P(('groups', 'rows')), parts along dimension 0, may hold values from -6 to 6
- conv_tiles: bfloat16 [16, 27, 512, 128], P('rows'), may hold values from -0.0390625 to 0.0390625
- up_tiles: bfloat16 [16, 9, 256, 128], P('rows'), may hold values from -0.0625 to 0.0625
Outputs:
- upsampled_tiles: bfloat16 [32, 256, 128], P(('groups', 'rows')), parts along dimension 0
The draws below stay inside these ranges and needn't reach their ends.
There are 2 independent parts, one for each index of `groups`. The reference program is written for one: setup_inputs(seed, part) draws one part's arguments, and reference() takes and returns one part's arrays. A program takes and returns all parts, laid end to end along the dimension named above; an argument that names none is the same for every part. Nothing has to cross between parts.
All inputs are finite; a program needn't handle non-finite values.
Results may differ from the reference program's by a relative error of at most 0.009.
Values may be sent and summed in bfloat16 or wider, within the bound.
A program may use at most 64 MiB of HBM per device.

```python
import jax
import jax.numpy as jnp

C = 1024
CO = 512
W = 64
SBLOCKS = 2
H = 4
V = 256
KI = 512
KO = 128
OB = 256
VB2 = 128
N_ROWS = 16


def level_of(key, extent, shards, least, top_value):
    def one(dim, shards_of):
        draws = jax.random.uniform(jax.random.fold_in(jax.random.fold_in(key, 6), dim), (shards_of,), jnp.float32, least / len(shards), top_value / len(shards))
        return jnp.repeat(jnp.exp(draws), extent[dim] // shards_of).reshape((-1,) + (1,) * (len(extent) - dim - 1))

    loudness = one(*shards[0])
    for cut in shards[1:]:
        loudness = loudness * one(*cut)
    return loudness


def bell_draw(own_key, dims, spread, limit, shards=(), held_as=jnp.bfloat16):
    entries = spread * jax.random.normal(own_key, dims, jnp.float32)
    if shards:
        entries = entries * level_of(own_key, dims, shards, -0.22, 0.18)
    return jnp.clip(entries, -limit, limit).astype(held_as)


def setup_inputs(seed: int = 0, part: int = 0) -> dict:
    streams_of = jax.random.split(jax.random.key(seed), 4)
    own_keys = jax.random.split(jax.random.fold_in(streams_of[3], part), 4)
    return {
        "frames": bell_draw(own_keys[0], (C, 3, V), 1.0, 6.0, ((0, 16),)),
        "conv_tiles": bell_draw(streams_of[1], (N_ROWS, 27, KI, KO), (27 * C) ** -0.5, 0.0390625, ((0, 16),)),
        "up_tiles": bell_draw(streams_of[2], (N_ROWS, 9, OB, KO), (9 * C) ** -0.5, 0.0625, ((0, 16),)),
    }


def shift_plane(planes, row_step, col_step):
    height = planes.shape[-2]
    width = planes.shape[-1]
    padded = jnp.pad(planes, [(0, 0)] * (planes.ndim - 2) + [(1, 1), (1, 1)])
    return padded[..., 1 + row_step:1 + row_step + height, 1 + col_step:1 + col_step + width]


def phase_groups(phase):
    if phase == 0:
        return [(-1, (0,)), (0, (1, 2))]
    return [(0, (0, 1)), (1, (2,))]


def reference(frames, conv_tiles, up_tiles):
    conv_weight = conv_tiles.reshape(SBLOCKS, 8, 27, KI, KO).transpose(2, 0, 3, 1, 4).reshape(27, C, C)
    volume = frames.reshape(C, 3, H, W)
    totals = jnp.zeros((C, V), jnp.float32)
    for kernel_tap in range(27):
        time_tap = kernel_tap // 9
        row_tap = (kernel_tap // 3) % 3
        col_tap = kernel_tap % 3
        plane = shift_plane(volume[:, time_tap], row_tap - 1, col_tap - 1).reshape(C, V)
        totals = totals + jnp.dot(conv_weight[kernel_tap].T, plane, preferred_element_type=jnp.float32)
    hidden = jax.nn.silu(totals).astype(jnp.bfloat16)
    hidden_planes = hidden.reshape(C, H, W)
    up_weight = up_tiles.reshape(SBLOCKS, 8, 9, OB, KO).transpose(2, 1, 4, 0, 3).reshape(9, C, CO)
    phase_rows = []
    for row_phase in range(2):
        phase_cols = []
        for col_phase in range(2):
            acc = jnp.zeros((CO, V), jnp.float32)
            for row_shift, row_taps in phase_groups(row_phase):
                for col_shift, col_taps in phase_groups(col_phase):
                    combined = jnp.zeros((C, CO), jnp.float32)
                    for row_tap in row_taps:
                        for col_tap in col_taps:
                            combined = combined + up_weight[3 * row_tap + col_tap].astype(jnp.float32)
                    combined = combined.astype(jnp.bfloat16)
                    plane = shift_plane(hidden_planes, row_shift, col_shift).reshape(C, V)
                    acc = acc + jnp.dot(combined.T, plane, preferred_element_type=jnp.float32)
            phase_cols.append(acc.reshape(CO, H, W))
        phase_rows.append(jnp.stack(phase_cols, 0))
    phased = jnp.stack(phase_rows, 0)
    result = phased.transpose(2, 3, 0, 4, 1).reshape(CO, 4 * V)
    rounded = result.astype(jnp.bfloat16)
    return rounded.reshape(SBLOCKS, OB, 8, VB2).transpose(0, 2, 1, 3).reshape(N_ROWS, OB, VB2)
```

```python
import jax
import jax.numpy as jnp
from jax import lax
from jax.experimental import pallas as pl
from jax.experimental.pallas import tpu as pltpu
from jax.sharding import PartitionSpec as P

W = 64


def partner_2(block, axis, stride):
    count = lax.axis_size(axis)
    route = []
    for low in range(count):
        high = low | 1 << stride
        if high != low and high < count:
            route += [(low, high), (high, low)]
    return lax.ppermute(block, axis, route)


def shift_plane(planes, row_step, col_step):
    height = planes.shape[-2]
    width = planes.shape[-1]
    padded = jnp.pad(planes, [(0, 0)] * (planes.ndim - 2) + [(1, 1), (1, 1)])
    return padded[..., 1 + row_step : 1 + row_step + height, 1 + col_step : 1 + col_step + width]


def phase_groups(phase):
    if phase == 0:
        return [(-1, (0,)), (0, (1, 2))]
    return [(0, (0, 1)), (1, (2,))]


def upper_side(device_index, level):
    return device_index >> level & 1 == 1


def collect_channels(pieces, device_index):
    for level in range(3):
        partner = partner_2(pieces, "rows", level)
        pieces = jnp.where(
            upper_side(device_index, level),
            jnp.concatenate([partner, pieces], 0),
            jnp.concatenate([pieces, partner], 0),
        )
    return pieces


def halve_partials(totals, device_index, levels):
    for level in levels:
        middle = totals.shape[1] // 2
        upper_half = upper_side(device_index, level)
        kept_part = jnp.where(upper_half, totals[:, middle:], totals[:, :middle])
        sent_part = jnp.where(upper_half, totals[:, :middle], totals[:, middle:])
        totals = kept_part + partner_2(sent_part, "rows", level)
    return totals


def halve_outputs(totals, device_index):
    for level in (2, 1, 0):
        middle = totals.shape[1] // 2
        upper_half = upper_side(device_index, level)
        kept_part = jnp.where(upper_half, totals[:, middle:], totals[:, :middle])
        sent_part = jnp.where(upper_half, totals[:, :middle], totals[:, middle:])
        totals = kept_part + partner_2(sent_part.astype(jnp.bfloat16), "rows", level).astype(
            sent_part.dtype
        )
    return totals


def on_device(frames, conv_tiles, up_tiles):
    device_index = lax.axis_index("rows")
    bit_count = lax.axis_size("rows").bit_length() - 1
    pieces = collect_channels(frames, device_index)
    in_channels = pieces.shape[0]
    voxels = pieces.shape[2]
    height = voxels // W
    volume = pieces.reshape(in_channels, 3, height, W)
    filters = conv_tiles.shape[3]
    partial_value = jnp.zeros((filters, voxels), jnp.float32)
    for time_tap in range(3):
        planes = []
        for spatial_tap in range(9):
            row_tap = spatial_tap // 3
            col_tap = spatial_tap % 3
            planes.append(
                shift_plane(volume[:, time_tap], row_tap - 1, col_tap - 1).reshape(
                    in_channels, voxels
                )
            )
        columns = jnp.concatenate(planes, 0)
        weights = conv_tiles[0, 9 * time_tap : 9 * time_tap + 9].reshape(9 * in_channels, filters)
        partial_value = partial_value + lax.dot_general(
            weights, columns, (((0,), (0,)), ((), ())), preferred_element_type=jnp.float32
        )
    summed = halve_partials(partial_value, device_index, list(range(bit_count - 1, 2, -1)))
    hidden_block = jax.nn.silu(summed).astype(jnp.bfloat16)
    for level in range(3, bit_count):
        partner = partner_2(hidden_block, "rows", level)
        hidden_block = jnp.where(
            upper_side(device_index, level),
            jnp.concatenate([partner, hidden_block], 1),
            jnp.concatenate([hidden_block, partner], 1),
        )
    hidden_planes = hidden_block.reshape(filters, height, W)
    up_weight = up_tiles[0].astype(jnp.float32)
    out_channels = up_weight.shape[1]
    phase_rows = []
    for row_phase in range(2):
        phase_cols = []
        for col_phase in range(2):
            weight_parts = []
            plane_parts = []
            for row_shift, row_taps in phase_groups(row_phase):
                for col_shift, col_taps in phase_groups(col_phase):
                    combined = jnp.zeros((out_channels, filters), jnp.float32)
                    for row_tap in row_taps:
                        for col_tap in col_taps:
                            combined = combined + up_weight[3 * row_tap + col_tap]
                    weight_parts.append(combined.astype(jnp.bfloat16))
                    plane_parts.append(
                        shift_plane(hidden_planes, row_shift, col_shift).reshape(filters, voxels)
                    )
            stacked_weight = jnp.concatenate(weight_parts, 1)
            stacked_planes = jnp.concatenate(plane_parts, 0)
            phase_out = jnp.dot(stacked_weight, stacked_planes, preferred_element_type=jnp.float32)
            phase_cols.append(phase_out.reshape(out_channels, height, W))
        phase_rows.append(jnp.stack(phase_cols, 0))
    phased = jnp.stack(phase_rows, 0)
    result = phased.transpose(2, 3, 0, 4, 1).reshape(out_channels, 4 * voxels)
    summed_out = halve_outputs(result, device_index)
    return summed_out.astype(jnp.bfloat16).reshape(1, out_channels, summed_out.shape[1])


MESH = pl.DeviceIdType.MESH


def fused_kernel(
    frames_ref, conv_hbm, up_hbm, out_ref,
    xg, wbuf, upbuf, pw, zacc, partial, pbuf, prx, hp, ownp, sbuf, crx, rbuf, rrx,
    lsem, gs, gr, ps, pr, cs_, cr, rs, rr,
):
    me = lax.axis_index("rows")
    f = lax.rem(me, 8)
    half = me // 8
    c = lax.rem(f, 2)
    y = lax.rem(f // 2, 2)
    z = f // 4
    dc, dy, dz = 1 - 2 * c, 2 - 4 * y, 4 - 8 * z
    pc, py, pz, pd = me + dc, me + dy, me + dz, me + dy + dz
    far = me + 8 - 16 * half
    shard, _, voxels = frames_ref.shape
    height = voxels // W
    depth = wbuf.shape[1] // 2
    filters = wbuf.shape[2]
    piece = shard // 2

    def weight_copy(k, which):
        rows = pl.ds(pl.multiple_of(which * depth, depth), depth)
        return pltpu.make_async_copy(conv_hbm.at[0, :, rows, :], wbuf.at[:, rows, :], lsem.at[k])

    w_near = weight_copy(0, z)
    w_far = weight_copy(1, 1 - z)
    up_copy = pltpu.make_async_copy(up_hbm.at[0], upbuf, lsem.at[2])

    barrier = pltpu.get_barrier_semaphore()
    for peer in (pc, py, pz, pd, far):
        pl.semaphore_signal(barrier, inc=1, device_id={"rows": peer}, device_id_type=MESH)
    w_near.start()
    up_copy.start()
    w_far.start()
    for a in range(3):
        xg[a, pl.ds(pl.multiple_of(f * shard, shard), shard), :] = frames_ref[:, a, :]
    pl.semaphore_wait(barrier, 5)

    def send(src, dst, ssem, rsem, k, peer):
        return pltpu.make_async_remote_copy(
            src_ref=src, dst_ref=dst, send_sem=ssem.at[k], recv_sem=rsem.at[k],
            device_id={"rows": peer}, device_id_type=MESH,
        )

    def gather(k, slot, part, peer):
        if part is None:
            view = xg.at[:, pl.ds(pl.multiple_of(slot * shard, shard), shard), :]
        else:
            view = xg.at[:, pl.ds(pl.multiple_of(slot * shard + part * piece, piece), piece), :]
        return send(view, view, gs, gr, k, peer)

    sy, sz, sd = f + dy, f + dz, f + dy + dz
    own_y0 = gather(0, f, 0, py)
    own_z1 = gather(1, f, 1, pz)
    own_y1 = gather(2, f, 1, py)
    own_z0 = gather(3, f, 0, pz)
    own_c = gather(4, f, None, pc)
    for copy in (own_y0, own_z1, own_c, own_y1, own_z0):
        copy.start()

    up_copy.wait()
    for p in range(2):
        for q in range(2):
            for k, (_, row_taps) in enumerate(phase_groups(p)):
                for l, (_, col_taps) in enumerate(phase_groups(q)):
                    total = None
                    for b in row_taps:
                        for e in col_taps:
                            tap = upbuf[3 * b + e].astype(jnp.float32)
                            total = tap if total is None else total + tap
                    at = (2 * k + l) * filters
                    pw[p, q, :, at : at + filters] = total.astype(jnp.bfloat16)

    own_y0.wait_recv()
    d_z0 = gather(5, sy, 0, pz)
    d_z0.start()
    y0_c = gather(6, sy, 0, pc)
    y0_c.start()
    own_z1.wait_recv()
    d_y1 = gather(7, sz, 1, py)
    d_y1.start()
    z1_c = gather(8, sz, 1, pc)
    z1_c.start()
    own_y1.wait_recv()
    y1_c = gather(9, sy, 1, pc)
    y1_c.start()
    own_z0.wait_recv()
    z0_c = gather(10, sz, 0, pc)
    z0_c.start()

    def conv_half(which, first):
        rows = pl.ds(pl.multiple_of(which * depth, depth), depth)
        xt = jnp.concatenate([xg[a, rows, :].T for a in range(3)], axis=1)
        for t in range(0, 9, 2):
            taps = [t, t + 1] if t + 1 < 9 else [t]
            rhs = jnp.concatenate(
                [jnp.concatenate([wbuf[9 * a + tap, rows, :] for a in range(3)], 0) for tap in taps], 1
            )
            got = jnp.dot(xt, rhs, preferred_element_type=jnp.float32)
            lanes = slice(t * filters, (t + len(taps)) * filters)
            if first:
                zacc[:, lanes] = got
            else:
                zacc[:, lanes] = zacc[:, lanes] + got

    own_c.wait_recv()
    y0_c.wait_recv()
    y1_c.wait_recv()
    w_near.wait()
    conv_half(z, True)

    d_z0.wait_recv()
    d0_c = gather(11, sd, 0, pc)
    d0_c.start()
    d_y1.wait_recv()
    d1_c = gather(12, sd, 1, pc)
    d1_c.start()
    z0_c.wait_recv()
    z1_c.wait_recv()
    w_far.wait()
    d0_c.wait_recv()
    d1_c.wait_recv()
    conv_half(1 - z, False)

    column = lax.rem(lax.broadcasted_iota(jnp.int32, (voxels, filters), 0), W)
    at_left = column == 0
    at_right = column == W - 1
    blank = jnp.zeros((W, filters), jnp.float32)
    sums = []
    for e in range(3):
        up_tap, mid_tap, low_tap = (
            zacc[:, (3 * b + e) * filters : (3 * b + e + 1) * filters] for b in range(3)
        )
        sums.append(
            mid_tap
            + jnp.concatenate([blank, up_tap[: voxels - W]], 0)
            + jnp.concatenate([low_tap[W:], blank], 0)
        )
    total = (
        sums[1]
        + jnp.where(at_left, 0.0, pltpu.roll(sums[0], 1, 0))
        + jnp.where(at_right, 0.0, pltpu.roll(sums[2], voxels - 1, 0))
    )
    pbuf[...] = total.astype(jnp.bfloat16)
    swap = send(pbuf, prx, ps, pr, 0, far)
    swap.start()
    partial[...] = total
    edge = jnp.zeros((W, filters), jnp.bfloat16)
    for s in range(3):
        hp[s, :W, :] = edge
        hp[s, W + voxels :, :] = edge
    swap.wait_recv()
    pre = partial[...] + prx[...].astype(jnp.float32)
    hidden = (pre / (1.0 + jnp.exp(-pre))).astype(jnp.bfloat16).astype(jnp.float32)
    inner = slice(W, W + voxels)
    hp[0, inner, :] = jnp.where(at_left, 0.0, pltpu.roll(hidden, 1, 0)).astype(jnp.bfloat16)
    hp[1, inner, :] = hidden.astype(jnp.bfloat16)
    hp[2, inner, :] = jnp.where(at_right, 0.0, pltpu.roll(hidden, voxels - 1, 0)).astype(jnp.bfloat16)

    def phase(p, target):
        for q in range(2):
            planes = jnp.concatenate(
                [
                    hp[q + l, pl.ds(pl.multiple_of((p + k) * W, W), voxels), :]
                    for k in range(2)
                    for l in range(2)
                ],
                1,
            )
            got = lax.dot_general(
                planes, pw[p, q], (((1,), (1,)), ((), ())), preferred_element_type=jnp.float32
            ).astype(target.dtype)
            for row in range(height):
                target[row, q * W : (q + 1) * W, :] = got[row * W : (row + 1) * W]

    here = 2 * z + y
    to_y = 2 * z + 1 - y
    to_z = 2 * (1 - z) + y
    to_d = 2 * (1 - z) + 1 - y
    phase(1 - c, sbuf)
    core = [send(sbuf.at[row], crx.at[row], cs_, cr, k, pc) for k, row in enumerate((to_d, to_z, to_y, here))]
    for copy in core:
        copy.start()
    phase(c, ownp)
    hops = []
    for k, (row, peer) in enumerate(((to_d, pd), (to_z, pz), (to_y, py))):
        core[k].wait_recv()
        rbuf[k] = (ownp[row] + crx[row].astype(jnp.float32)).astype(jnp.bfloat16)
        hop = send(rbuf.at[k], rrx.at[k], rs, rr, k, peer)
        hop.start()
        hops.append(hop)
    core[3].wait_recv()
    final = ownp[here] + crx[here].astype(jnp.float32)
    for k in (2, 1, 0):
        hops[k].wait_recv()
        final = final + rrx[k].astype(jnp.float32)
    from_row = lax.broadcasted_iota(jnp.int32, (2 * W, 2 * W), 0)
    to_col = lax.broadcasted_iota(jnp.int32, (2 * W, 2 * W), 1)
    place = (to_col == 2 * lax.rem(from_row, W) + from_row // W).astype(jnp.float32).astype(jnp.bfloat16)
    out_ref[0] = lax.dot_general(
        final.astype(jnp.bfloat16), place, (((0,), (0,)), ((), ())), preferred_element_type=jnp.float32
    ).astype(jnp.bfloat16)
    for copy in (
        own_y0, own_z1, own_y1, own_z0, own_c, d_z0, y0_c, d_y1, z1_c, y1_c, z0_c, d0_c, d1_c,
        swap, *core, *hops,
    ):
        copy.wait_send()


def fused(frames, conv_tiles, up_tiles):
    shard, _, voxels = frames.shape
    _, taps, depth, filters = conv_tiles.shape
    _, up_taps, outs, _ = up_tiles.shape
    height = voxels // W
    tile = 2 * W
    bf, f32 = jnp.bfloat16, jnp.float32
    dma = pltpu.SemaphoreType.DMA
    return pl.pallas_call(
        fused_kernel,
        out_shape=jax.ShapeDtypeStruct((1, outs, tile), bf),
        in_specs=[
            pl.BlockSpec(memory_space=pltpu.VMEM),
            pl.BlockSpec(memory_space=pl.ANY),
            pl.BlockSpec(memory_space=pl.ANY),
        ],
        out_specs=pl.BlockSpec(memory_space=pltpu.VMEM),
        scratch_shapes=[
            pltpu.VMEM((3, depth, voxels), bf),
            pltpu.VMEM((taps, depth, filters), bf),
            pltpu.VMEM((up_taps, outs, filters), bf),
            pltpu.VMEM((2, 2, outs, 4 * filters), bf),
            pltpu.VMEM((voxels, 9 * filters), f32),
            pltpu.VMEM((voxels, filters), f32),
            pltpu.VMEM((voxels, filters), bf),
            pltpu.VMEM((voxels, filters), bf),
            pltpu.VMEM((3, voxels + 2 * W, filters), bf),
            pltpu.VMEM((height, tile, outs), f32),
            pltpu.VMEM((height, tile, outs), bf),
            pltpu.VMEM((height, tile, outs), bf),
            pltpu.VMEM((3, tile, outs), bf),
            pltpu.VMEM((3, tile, outs), bf),
            dma((3,)),
            dma((13,)), dma((13,)),
            dma((1,)), dma((1,)),
            dma((4,)), dma((4,)),
            dma((3,)), dma((3,)),
        ],
        compiler_params=pltpu.CompilerParams(collective_id=0, has_side_effects=True),
    )(frames, conv_tiles, up_tiles)


def route(frames, conv_tiles, up_tiles):
    blocks = lax.axis_size("rows") // 8
    tile_rows = frames.shape[2] // W // 4
    if blocks == 2 and tile_rows == 1 and frames.shape[0] * 8 == conv_tiles.shape[2]:
        return fused(frames, conv_tiles, up_tiles)
    return on_device(frames, conv_tiles, up_tiles)


def solution(mesh):
    return jax.shard_map(
        route,
        mesh=mesh,
        in_specs=(
            P(("groups", "rows"), None, None),
            P("rows", None, None, None),
            P("rows", None, None, None),
        ),
        out_specs=P(("groups", "rows"), None, None),
        check_vma=False,
    )
```

```python
import jax
import jax.numpy as jnp
from jax import lax
from jax.experimental import pallas as pl
from jax.experimental.pallas import tpu as pltpu
from jax.sharding import PartitionSpec as P

W = 64


def partner_2(block, axis, stride):
    count = lax.axis_size(axis)
    route = []
    for low in range(count):
        high = low | 1 << stride
        if high != low and high < count:
            route += [(low, high), (high, low)]
    return lax.ppermute(block, axis, route)


def shift_plane(planes, row_step, col_step):
    height = planes.shape[-2]
    width = planes.shape[-1]
    padded = jnp.pad(planes, [(0, 0)] * (planes.ndim - 2) + [(1, 1), (1, 1)])
    return padded[..., 1 + row_step : 1 + row_step + height, 1 + col_step : 1 + col_step + width]


def phase_groups(phase):
    if phase == 0:
        return [(-1, (0,)), (0, (1, 2))]
    return [(0, (0, 1)), (1, (2,))]


def upper_side(device_index, level):
    return device_index >> level & 1 == 1


def collect_channels(pieces, device_index):
    for level in range(3):
        partner = partner_2(pieces, "rows", level)
        pieces = jnp.where(
            upper_side(device_index, level),
            jnp.concatenate([partner, pieces], 0),
            jnp.concatenate([pieces, partner], 0),
        )
    return pieces


def halve_partials(totals, device_index, levels):
    for level in levels:
        middle = totals.shape[1] // 2
        upper_half = upper_side(device_index, level)
        kept_part = jnp.where(upper_half, totals[:, middle:], totals[:, :middle])
        sent_part = jnp.where(upper_half, totals[:, :middle], totals[:, middle:])
        totals = kept_part + partner_2(sent_part, "rows", level)
    return totals


def halve_outputs(totals, device_index):
    for level in (2, 1, 0):
        middle = totals.shape[1] // 2
        upper_half = upper_side(device_index, level)
        kept_part = jnp.where(upper_half, totals[:, middle:], totals[:, :middle])
        sent_part = jnp.where(upper_half, totals[:, :middle], totals[:, middle:])
        totals = kept_part + partner_2(sent_part.astype(jnp.bfloat16), "rows", level).astype(
            sent_part.dtype
        )
    return totals


def on_device(frames, conv_tiles, up_tiles):
    device_index = lax.axis_index("rows")
    bit_count = lax.axis_size("rows").bit_length() - 1
    pieces = collect_channels(frames, device_index)
    in_channels = pieces.shape[0]
    voxels = pieces.shape[2]
    height = voxels // W
    volume = pieces.reshape(in_channels, 3, height, W)
    filters = conv_tiles.shape[3]
    partial_value = jnp.zeros((filters, voxels), jnp.float32)
    for time_tap in range(3):
        planes = []
        for spatial_tap in range(9):
            row_tap = spatial_tap // 3
            col_tap = spatial_tap % 3
            planes.append(
                shift_plane(volume[:, time_tap], row_tap - 1, col_tap - 1).reshape(
                    in_channels, voxels
                )
            )
        columns = jnp.concatenate(planes, 0)
        weights = conv_tiles[0, 9 * time_tap : 9 * time_tap + 9].reshape(9 * in_channels, filters)
        partial_value = partial_value + lax.dot_general(
            weights, columns, (((0,), (0,)), ((), ())), preferred_element_type=jnp.float32
        )
    summed = halve_partials(partial_value, device_index, list(range(bit_count - 1, 2, -1)))
    hidden_block = jax.nn.silu(summed).astype(jnp.bfloat16)
    for level in range(3, bit_count):
        partner = partner_2(hidden_block, "rows", level)
        hidden_block = jnp.where(
            upper_side(device_index, level),
            jnp.concatenate([partner, hidden_block], 1),
            jnp.concatenate([hidden_block, partner], 1),
        )
    hidden_planes = hidden_block.reshape(filters, height, W)
    up_weight = up_tiles[0].astype(jnp.float32)
    out_channels = up_weight.shape[1]
    phase_rows = []
    for row_phase in range(2):
        phase_cols = []
        for col_phase in range(2):
            weight_parts = []
            plane_parts = []
            for row_shift, row_taps in phase_groups(row_phase):
                for col_shift, col_taps in phase_groups(col_phase):
                    combined = jnp.zeros((out_channels, filters), jnp.float32)
                    for row_tap in row_taps:
                        for col_tap in col_taps:
                            combined = combined + up_weight[3 * row_tap + col_tap]
                    weight_parts.append(combined.astype(jnp.bfloat16))
                    plane_parts.append(
                        shift_plane(hidden_planes, row_shift, col_shift).reshape(filters, voxels)
                    )
            stacked_weight = jnp.concatenate(weight_parts, 1)
            stacked_planes = jnp.concatenate(plane_parts, 0)
            phase_out = jnp.dot(stacked_weight, stacked_planes, preferred_element_type=jnp.float32)
            phase_cols.append(phase_out.reshape(out_channels, height, W))
        phase_rows.append(jnp.stack(phase_cols, 0))
    phased = jnp.stack(phase_rows, 0)
    result = phased.transpose(2, 3, 0, 4, 1).reshape(out_channels, 4 * voxels)
    summed_out = halve_outputs(result, device_index)
    return summed_out.astype(jnp.bfloat16).reshape(1, out_channels, summed_out.shape[1])


MESH = pl.DeviceIdType.MESH


def fused_kernel(
    frames_ref, conv_hbm, up_hbm, out_ref,
    xg, wbuf, upbuf, pw, zacc, partial, pbuf, prx, hp, ownp, sbuf, crx, rbuf, rrx,
    lsem, gs, gr, ps, pr, cs_, cr, rs, rr,
):
    me = lax.axis_index("rows")
    f = lax.rem(me, 8)
    half = me // 8
    c = lax.rem(f, 2)
    y = lax.rem(f // 2, 2)
    z = f // 4
    dc, dy, dz = 1 - 2 * c, 2 - 4 * y, 4 - 8 * z
    pc, py, pz, pd = me + dc, me + dy, me + dz, me + dy + dz
    far = me + 8 - 16 * half
    _, shard, voxels = frames_ref.shape
    height = voxels // W
    depth = wbuf.shape[1] // 2
    filters = wbuf.shape[2]
    piece = shard // 2

    def weight_copy(k, which):
        rows = pl.ds(pl.multiple_of(which * depth, depth), depth)
        return pltpu.make_async_copy(conv_hbm.at[0, :, rows, :], wbuf.at[:, rows, :], lsem.at[k])

    w_near = weight_copy(0, z)
    w_far = weight_copy(1, 1 - z)
    up_copy = pltpu.make_async_copy(up_hbm.at[0], upbuf, lsem.at[2])

    own_copy = pltpu.make_async_copy(
        frames_ref, xg.at[:, pl.ds(pl.multiple_of(f * shard, shard), shard), :], lsem.at[3]
    )
    own_copy.start()
    barrier = pltpu.get_barrier_semaphore()
    for peer in (pc, py, pz, pd, far):
        pl.semaphore_signal(barrier, inc=1, device_id={"rows": peer}, device_id_type=MESH)
    w_near.start()
    up_copy.start()
    w_far.start()
    pl.semaphore_wait(barrier, 5)
    own_copy.wait()

    def send(src, dst, ssem, rsem, k, peer):
        return pltpu.make_async_remote_copy(
            src_ref=src, dst_ref=dst, send_sem=ssem.at[k], recv_sem=rsem.at[k],
            device_id={"rows": peer}, device_id_type=MESH,
        )

    def gather(k, slot, part, peer):
        if part is None:
            view = xg.at[:, pl.ds(pl.multiple_of(slot * shard, shard), shard), :]
        else:
            view = xg.at[:, pl.ds(pl.multiple_of(slot * shard + part * piece, piece), piece), :]
        return send(view, view, gs, gr, k, peer)

    sy, sz, sd = f + dy, f + dz, f + dy + dz
    own_y0 = gather(0, f, 0, py)
    own_z1 = gather(1, f, 1, pz)
    own_y1 = gather(2, f, 1, py)
    own_z0 = gather(3, f, 0, pz)
    own_c = gather(4, f, None, pc)
    for copy in (own_y0, own_z1, own_c, own_y1, own_z0):
        copy.start()

    up_copy.wait()
    for p in range(2):
        for q in range(2):
            for k, (_, row_taps) in enumerate(phase_groups(p)):
                for l, (_, col_taps) in enumerate(phase_groups(q)):
                    total = None
                    for b in row_taps:
                        for e in col_taps:
                            tap = upbuf[3 * b + e].astype(jnp.float32)
                            total = tap if total is None else total + tap
                    at = (2 * k + l) * filters
                    pw[p, q, :, at : at + filters] = total.astype(jnp.bfloat16)

    own_y0.wait_recv()
    d_z0 = gather(5, sy, 0, pz)
    d_z0.start()
    y0_c = gather(6, sy, 0, pc)
    y0_c.start()
    own_z1.wait_recv()
    d_y1 = gather(7, sz, 1, py)
    d_y1.start()
    z1_c = gather(8, sz, 1, pc)
    z1_c.start()
    own_y1.wait_recv()
    y1_c = gather(9, sy, 1, pc)
    y1_c.start()
    own_z0.wait_recv()
    z0_c = gather(10, sz, 0, pc)
    z0_c.start()

    def conv_half(which, first):
        rows = pl.ds(pl.multiple_of(which * depth, depth), depth)
        xt = jnp.concatenate([xg[a, rows, :].T for a in range(3)], axis=1)
        for t in range(0, 9, 2):
            taps = [t, t + 1] if t + 1 < 9 else [t]
            rhs = jnp.concatenate(
                [jnp.concatenate([wbuf[9 * a + tap, rows, :] for a in range(3)], 0) for tap in taps], 1
            )
            got = jnp.dot(xt, rhs, preferred_element_type=jnp.float32)
            lanes = slice(t * filters, (t + len(taps)) * filters)
            if first:
                zacc[:, lanes] = got
            else:
                zacc[:, lanes] = zacc[:, lanes] + got

    own_c.wait_recv()
    y0_c.wait_recv()
    y1_c.wait_recv()
    w_near.wait()
    conv_half(z, True)

    d_z0.wait_recv()
    d0_c = gather(11, sd, 0, pc)
    d0_c.start()
    d_y1.wait_recv()
    d1_c = gather(12, sd, 1, pc)
    d1_c.start()
    z0_c.wait_recv()
    z1_c.wait_recv()
    w_far.wait()
    d0_c.wait_recv()
    d1_c.wait_recv()
    conv_half(1 - z, False)

    column = lax.rem(lax.broadcasted_iota(jnp.int32, (voxels, filters), 0), W)
    at_left = column == 0
    at_right = column == W - 1
    blank = jnp.zeros((W, filters), jnp.float32)
    sums = []
    for e in range(3):
        up_tap, mid_tap, low_tap = (
            zacc[:, (3 * b + e) * filters : (3 * b + e + 1) * filters] for b in range(3)
        )
        sums.append(
            mid_tap
            + jnp.concatenate([blank, up_tap[: voxels - W]], 0)
            + jnp.concatenate([low_tap[W:], blank], 0)
        )
    total = (
        sums[1]
        + jnp.where(at_left, 0.0, pltpu.roll(sums[0], 1, 0))
        + jnp.where(at_right, 0.0, pltpu.roll(sums[2], voxels - 1, 0))
    )
    pbuf[...] = total.astype(jnp.bfloat16)
    swap = send(pbuf, prx, ps, pr, 0, far)
    swap.start()
    partial[...] = total
    edge = jnp.zeros((W, filters), jnp.bfloat16)
    for s in range(3):
        hp[s, :W, :] = edge
        hp[s, W + voxels :, :] = edge
    swap.wait_recv()
    pre = partial[...] + prx[...].astype(jnp.float32)
    hidden = (pre / (1.0 + jnp.exp(-pre))).astype(jnp.bfloat16).astype(jnp.float32)
    inner = slice(W, W + voxels)
    hp[0, inner, :] = jnp.where(at_left, 0.0, pltpu.roll(hidden, 1, 0)).astype(jnp.bfloat16)
    hp[1, inner, :] = hidden.astype(jnp.bfloat16)
    hp[2, inner, :] = jnp.where(at_right, 0.0, pltpu.roll(hidden, voxels - 1, 0)).astype(jnp.bfloat16)

    def phase(p, target):
        for q in range(2):
            planes = jnp.concatenate(
                [
                    hp[q + l, pl.ds(pl.multiple_of((p + k) * W, W), voxels), :]
                    for k in range(2)
                    for l in range(2)
                ],
                1,
            )
            got = lax.dot_general(
                planes, pw[p, q], (((1,), (1,)), ((), ())), preferred_element_type=jnp.float32
            ).astype(target.dtype)
            for row in range(height):
                target[row, q * W : (q + 1) * W, :] = got[row * W : (row + 1) * W]

    here = 2 * z + y
    to_y = 2 * z + 1 - y
    to_z = 2 * (1 - z) + y
    to_d = 2 * (1 - z) + 1 - y
    phase(1 - c, sbuf)
    core = [send(sbuf.at[row], crx.at[row], cs_, cr, k, pc) for k, row in enumerate((to_d, to_z, to_y, here))]
    for copy in core:
        copy.start()
    phase(c, ownp)
    hops = []
    for k, (row, peer) in enumerate(((to_d, pd), (to_z, pz), (to_y, py))):
        core[k].wait_recv()
        rbuf[k] = (ownp[row] + crx[row].astype(jnp.float32)).astype(jnp.bfloat16)
        hop = send(rbuf.at[k], rrx.at[k], rs, rr, k, peer)
        hop.start()
        hops.append(hop)
    core[3].wait_recv()
    final = ownp[here] + crx[here].astype(jnp.float32)
    for k in (2, 1, 0):
        hops[k].wait_recv()
        final = final + rrx[k].astype(jnp.float32)
    from_row = lax.broadcasted_iota(jnp.int32, (2 * W, 2 * W), 0)
    to_col = lax.broadcasted_iota(jnp.int32, (2 * W, 2 * W), 1)
    place = (to_col == 2 * lax.rem(from_row, W) + from_row // W).astype(jnp.float32).astype(jnp.bfloat16)
    out_ref[0] = lax.dot_general(
        final.astype(jnp.bfloat16), place, (((0,), (0,)), ((), ())), preferred_element_type=jnp.float32
    )
    for copy in (
        own_y0, own_z1, own_y1, own_z0, own_c, d_z0, y0_c, d_y1, z1_c, y1_c, z0_c, d0_c, d1_c,
        swap, *core, *hops,
    ):
        copy.wait_send()


def fused(frames, conv_tiles, up_tiles):
    shard, _, voxels = frames.shape
    _, taps, depth, filters = conv_tiles.shape
    _, up_taps, outs, _ = up_tiles.shape
    height = voxels // W
    tile = 2 * W
    bf, f32 = jnp.bfloat16, jnp.float32
    dma = pltpu.SemaphoreType.DMA
    return pl.pallas_call(
        fused_kernel,
        out_shape=jax.ShapeDtypeStruct((1, outs, tile), f32),
        in_specs=[
            pl.BlockSpec(memory_space=pl.ANY),
            pl.BlockSpec(memory_space=pl.ANY),
            pl.BlockSpec(memory_space=pl.ANY),
        ],
        out_specs=pl.BlockSpec(memory_space=pltpu.VMEM),
        scratch_shapes=[
            pltpu.VMEM((3, depth, voxels), bf),
            pltpu.VMEM((taps, depth, filters), bf),
            pltpu.VMEM((up_taps, outs, filters), bf),
            pltpu.VMEM((2, 2, outs, 4 * filters), bf),
            pltpu.VMEM((voxels, 9 * filters), f32),
            pltpu.VMEM((voxels, filters), f32),
            pltpu.VMEM((voxels, filters), bf),
            pltpu.VMEM((voxels, filters), bf),
            pltpu.VMEM((3, voxels + 2 * W, filters), bf),
            pltpu.VMEM((height, tile, outs), f32),
            pltpu.VMEM((height, tile, outs), bf),
            pltpu.VMEM((height, tile, outs), bf),
            pltpu.VMEM((3, tile, outs), bf),
            pltpu.VMEM((3, tile, outs), bf),
            dma((4,)),
            dma((13,)), dma((13,)),
            dma((1,)), dma((1,)),
            dma((4,)), dma((4,)),
            dma((3,)), dma((3,)),
        ],
        compiler_params=pltpu.CompilerParams(collective_id=0, has_side_effects=True),
    )(frames.transpose(1, 0, 2), conv_tiles, up_tiles).astype(bf)


def route(frames, conv_tiles, up_tiles):
    blocks = lax.axis_size("rows") // 8
    tile_rows = frames.shape[2] // W // 4
    if blocks == 2 and tile_rows == 1 and frames.shape[0] * 8 == conv_tiles.shape[2]:
        return fused(frames, conv_tiles, up_tiles)
    return on_device(frames, conv_tiles, up_tiles)


def solution(mesh):
    return jax.shard_map(
        route,
        mesh=mesh,
        in_specs=(
            P(("groups", "rows"), None, None),
            P("rows", None, None, None),
            P("rows", None, None, None),
        ),
        out_specs=P(("groups", "rows"), None, None),
        check_vma=False,
    )
```

```python
import jax
import jax.numpy as jnp
from jax import lax
from jax.experimental import pallas as pl
from jax.experimental.pallas import tpu as pltpu
from jax.sharding import PartitionSpec as P

W = 64


def partner_2(block, axis, stride):
    count = lax.axis_size(axis)
    route = []
    for low in range(count):
        high = low | 1 << stride
        if high != low and high < count:
            route += [(low, high), (high, low)]
    return lax.ppermute(block, axis, route)


def shift_plane(planes, row_step, col_step):
    height = planes.shape[-2]
    width = planes.shape[-1]
    padded = jnp.pad(planes, [(0, 0)] * (planes.ndim - 2) + [(1, 1), (1, 1)])
    return padded[..., 1 + row_step : 1 + row_step + height, 1 + col_step : 1 + col_step + width]


def phase_groups(phase):
    if phase == 0:
        return [(-1, (0,)), (0, (1, 2))]
    return [(0, (0, 1)), (1, (2,))]


def upper_side(device_index, level):
    return device_index >> level & 1 == 1


def collect_channels(pieces, device_index):
    for level in range(3):
        partner = partner_2(pieces, "rows", level)
        pieces = jnp.where(
            upper_side(device_index, level),
            jnp.concatenate([partner, pieces], 0),
            jnp.concatenate([pieces, partner], 0),
        )
    return pieces


def halve_partials(totals, device_index, levels):
    for level in levels:
        middle = totals.shape[1] // 2
        upper_half = upper_side(device_index, level)
        kept_part = jnp.where(upper_half, totals[:, middle:], totals[:, :middle])
        sent_part = jnp.where(upper_half, totals[:, :middle], totals[:, middle:])
        totals = kept_part + partner_2(sent_part, "rows", level)
    return totals


def halve_outputs(totals, device_index):
    for level in (2, 1, 0):
        middle = totals.shape[1] // 2
        upper_half = upper_side(device_index, level)
        kept_part = jnp.where(upper_half, totals[:, middle:], totals[:, :middle])
        sent_part = jnp.where(upper_half, totals[:, :middle], totals[:, middle:])
        totals = kept_part + partner_2(sent_part.astype(jnp.bfloat16), "rows", level).astype(
            sent_part.dtype
        )
    return totals


def on_device(frames, conv_tiles, up_tiles):
    device_index = lax.axis_index("rows")
    bit_count = lax.axis_size("rows").bit_length() - 1
    pieces = collect_channels(frames, device_index)
    in_channels = pieces.shape[0]
    voxels = pieces.shape[2]
    height = voxels // W
    volume = pieces.reshape(in_channels, 3, height, W)
    filters = conv_tiles.shape[3]
    partial_value = jnp.zeros((filters, voxels), jnp.float32)
    for time_tap in range(3):
        planes = []
        for spatial_tap in range(9):
            row_tap = spatial_tap // 3
            col_tap = spatial_tap % 3
            planes.append(
                shift_plane(volume[:, time_tap], row_tap - 1, col_tap - 1).reshape(
                    in_channels, voxels
                )
            )
        columns = jnp.concatenate(planes, 0)
        weights = conv_tiles[0, 9 * time_tap : 9 * time_tap + 9].reshape(9 * in_channels, filters)
        partial_value = partial_value + lax.dot_general(
            weights, columns, (((0,), (0,)), ((), ())), preferred_element_type=jnp.float32
        )
    summed = halve_partials(partial_value, device_index, list(range(bit_count - 1, 2, -1)))
    hidden_block = jax.nn.silu(summed).astype(jnp.bfloat16)
    for level in range(3, bit_count):
        partner = partner_2(hidden_block, "rows", level)
        hidden_block = jnp.where(
            upper_side(device_index, level),
            jnp.concatenate([partner, hidden_block], 1),
            jnp.concatenate([hidden_block, partner], 1),
        )
    hidden_planes = hidden_block.reshape(filters, height, W)
    up_weight = up_tiles[0].astype(jnp.float32)
    out_channels = up_weight.shape[1]
    phase_rows = []
    for row_phase in range(2):
        phase_cols = []
        for col_phase in range(2):
            weight_parts = []
            plane_parts = []
            for row_shift, row_taps in phase_groups(row_phase):
                for col_shift, col_taps in phase_groups(col_phase):
                    combined = jnp.zeros((out_channels, filters), jnp.float32)
                    for row_tap in row_taps:
                        for col_tap in col_taps:
                            combined = combined + up_weight[3 * row_tap + col_tap]
                    weight_parts.append(combined.astype(jnp.bfloat16))
                    plane_parts.append(
                        shift_plane(hidden_planes, row_shift, col_shift).reshape(filters, voxels)
                    )
            stacked_weight = jnp.concatenate(weight_parts, 1)
            stacked_planes = jnp.concatenate(plane_parts, 0)
            phase_out = jnp.dot(stacked_weight, stacked_planes, preferred_element_type=jnp.float32)
            phase_cols.append(phase_out.reshape(out_channels, height, W))
        phase_rows.append(jnp.stack(phase_cols, 0))
    phased = jnp.stack(phase_rows, 0)
    result = phased.transpose(2, 3, 0, 4, 1).reshape(out_channels, 4 * voxels)
    summed_out = halve_outputs(result, device_index)
    return summed_out.astype(jnp.bfloat16).reshape(1, out_channels, summed_out.shape[1])


MESH = pl.DeviceIdType.MESH


def fused_kernel(
    frames_ref, conv_hbm, up_hbm, out_ref,
    xg, wbuf, upbuf, pw, zacc, partial, pbuf, prx, hp, ownp, sbuf, crx, rbuf, rrx,
    lsem, gs, gr, ps, pr, cs_, cr, rs, rr, ready,
):
    me = lax.axis_index("rows")
    f = lax.rem(me, 8)
    half = me // 8
    c = lax.rem(f, 2)
    y = lax.rem(f // 2, 2)
    z = f // 4
    dc, dy, dz = 1 - 2 * c, 2 - 4 * y, 4 - 8 * z
    pc, py, pz, pd = me + dc, me + dy, me + dz, me + dy + dz
    far = me + 8 - 16 * half
    _, shard, voxels = frames_ref.shape
    height = voxels // W
    depth = wbuf.shape[1] // 2
    filters = wbuf.shape[2]
    piece = shard // 2

    def weight_copy(k, which):
        rows = pl.ds(pl.multiple_of(which * depth, depth), depth)
        return pltpu.make_async_copy(conv_hbm.at[0, :, rows, :], wbuf.at[:, rows, :], lsem.at[k])

    w_near = weight_copy(0, z)
    w_far = weight_copy(1, 1 - z)
    up_copy = pltpu.make_async_copy(up_hbm.at[0], upbuf, lsem.at[2])

    own_copy = pltpu.make_async_copy(
        frames_ref, xg.at[:, pl.ds(pl.multiple_of(f * shard, shard), shard), :], lsem.at[3]
    )
    own_copy.start()
    barrier = pltpu.get_barrier_semaphore()
    for peer in (pc, py, pz):
        pl.semaphore_signal(barrier, inc=1, device_id={"rows": peer}, device_id_type=MESH)
    inner_chip = lax.rem(z + half, 2)
    middle = inner_chip == 1
    across = me + 4 - 8 * half

    @pl.when(middle)
    def _():
        pl.semaphore_signal(barrier, inc=1, device_id={"rows": across}, device_id_type=MESH)

    w_near.start()
    up_copy.start()
    w_far.start()
    pl.semaphore_wait(barrier, 3 + inner_chip)

    @pl.when(middle)
    def _():
        pl.semaphore_signal(ready, inc=1, device_id={"rows": across}, device_id_type=MESH)

    own_copy.wait()

    def send(src, dst, ssem, rsem, k, peer):
        return pltpu.make_async_remote_copy(
            src_ref=src, dst_ref=dst, send_sem=ssem.at[k], recv_sem=rsem.at[k],
            device_id={"rows": peer}, device_id_type=MESH,
        )

    def gather(k, slot, part, peer):
        if part is None:
            view = xg.at[:, pl.ds(pl.multiple_of(slot * shard, shard), shard), :]
        else:
            view = xg.at[:, pl.ds(pl.multiple_of(slot * shard + part * piece, piece), piece), :]
        return send(view, view, gs, gr, k, peer)

    sy, sz, sd = f + dy, f + dz, f + dy + dz
    own_y0 = gather(0, f, 0, py)
    own_z1 = gather(1, f, 1, pz)
    own_y1 = gather(2, f, 1, py)
    own_z0 = gather(3, f, 0, pz)
    own_c = gather(4, f, None, pc)
    for copy in (own_y0, own_z1, own_c, own_y1, own_z0):
        copy.start()

    up_copy.wait()
    for p in range(2):
        for q in range(2):
            for k, (_, row_taps) in enumerate(phase_groups(p)):
                for l, (_, col_taps) in enumerate(phase_groups(q)):
                    total = None
                    for b in row_taps:
                        for e in col_taps:
                            tap = upbuf[3 * b + e].astype(jnp.float32)
                            total = tap if total is None else total + tap
                    at = (2 * k + l) * filters
                    pw[p, q, :, at : at + filters] = total.astype(jnp.bfloat16)

    own_y0.wait_recv()
    d_z0 = gather(5, sy, 0, pz)
    d_z0.start()
    y0_c = gather(6, sy, 0, pc)
    y0_c.start()
    own_z1.wait_recv()
    d_y1 = gather(7, sz, 1, py)
    d_y1.start()
    z1_c = gather(8, sz, 1, pc)
    z1_c.start()
    own_y1.wait_recv()
    y1_c = gather(9, sy, 1, pc)
    y1_c.start()
    own_z0.wait_recv()
    z0_c = gather(10, sz, 0, pc)
    z0_c.start()

    def conv_half(which, first):
        rows = pl.ds(pl.multiple_of(which * depth, depth), depth)
        xt = jnp.concatenate([xg[a, rows, :].T for a in range(3)], axis=1)
        for t in range(0, 9, 2):
            taps = [t, t + 1] if t + 1 < 9 else [t]
            rhs = jnp.concatenate(
                [jnp.concatenate([wbuf[9 * a + tap, rows, :] for a in range(3)], 0) for tap in taps], 1
            )
            got = jnp.dot(xt, rhs, preferred_element_type=jnp.float32)
            lanes = slice(t * filters, (t + len(taps)) * filters)
            if first:
                zacc[:, lanes] = got
            else:
                zacc[:, lanes] = zacc[:, lanes] + got

    own_c.wait_recv()
    y0_c.wait_recv()
    y1_c.wait_recv()
    w_near.wait()
    conv_half(z, True)

    d_z0.wait_recv()
    d0_c = gather(11, sd, 0, pc)
    d0_c.start()
    d_y1.wait_recv()
    d1_c = gather(12, sd, 1, pc)
    d1_c.start()
    z0_c.wait_recv()
    z1_c.wait_recv()
    w_far.wait()
    d0_c.wait_recv()
    d1_c.wait_recv()
    conv_half(1 - z, False)

    column = lax.rem(lax.broadcasted_iota(jnp.int32, (voxels, filters), 0), W)
    at_left = column == 0
    at_right = column == W - 1
    blank = jnp.zeros((W, filters), jnp.float32)
    sums = []
    for e in range(3):
        up_tap, mid_tap, low_tap = (
            zacc[:, (3 * b + e) * filters : (3 * b + e + 1) * filters] for b in range(3)
        )
        sums.append(
            mid_tap
            + jnp.concatenate([blank, up_tap[: voxels - W]], 0)
            + jnp.concatenate([low_tap[W:], blank], 0)
        )
    total = (
        sums[1]
        + jnp.where(at_left, 0.0, pltpu.roll(sums[0], 1, 0))
        + jnp.where(at_right, 0.0, pltpu.roll(sums[2], voxels - 1, 0))
    )
    pbuf[...] = total.astype(jnp.bfloat16)
    swap = send(pbuf, prx, ps, pr, 0, far)

    @pl.when(middle)
    def _():
        pl.semaphore_wait(ready, 1)

    swap.start()
    partial[...] = total
    edge = jnp.zeros((W, filters), jnp.bfloat16)
    for s in range(3):
        hp[s, :W, :] = edge
        hp[s, W + voxels :, :] = edge
    swap.wait_recv()
    pre = partial[...] + prx[...].astype(jnp.float32)
    hidden = (pre / (1.0 + jnp.exp(-pre))).astype(jnp.bfloat16).astype(jnp.float32)
    inner = slice(W, W + voxels)
    hp[0, inner, :] = jnp.where(at_left, 0.0, pltpu.roll(hidden, 1, 0)).astype(jnp.bfloat16)
    hp[1, inner, :] = hidden.astype(jnp.bfloat16)
    hp[2, inner, :] = jnp.where(at_right, 0.0, pltpu.roll(hidden, voxels - 1, 0)).astype(jnp.bfloat16)

    def phase(p, target):
        for q in range(2):
            planes = jnp.concatenate(
                [
                    hp[q + l, pl.ds(pl.multiple_of((p + k) * W, W), voxels), :]
                    for k in range(2)
                    for l in range(2)
                ],
                1,
            )
            got = lax.dot_general(
                planes, pw[p, q], (((1,), (1,)), ((), ())), preferred_element_type=jnp.float32
            ).astype(target.dtype)
            for row in range(height):
                target[row, q * W : (q + 1) * W, :] = got[row * W : (row + 1) * W]

    here = 2 * z + y
    to_y = 2 * z + 1 - y
    to_z = 2 * (1 - z) + y
    to_d = 2 * (1 - z) + 1 - y
    phase(1 - c, sbuf)
    core = [send(sbuf.at[row], crx.at[row], cs_, cr, k, pc) for k, row in enumerate((to_d, to_z, to_y, here))]
    for copy in core:
        copy.start()
    phase(c, ownp)
    hops = []
    for k, (row, peer) in enumerate(((to_d, pd), (to_z, pz), (to_y, py))):
        core[k].wait_recv()
        rbuf[k] = (ownp[row] + crx[row].astype(jnp.float32)).astype(jnp.bfloat16)
        hop = send(rbuf.at[k], rrx.at[k], rs, rr, k, peer)
        hop.start()
        hops.append(hop)
    core[3].wait_recv()
    final = ownp[here] + crx[here].astype(jnp.float32)
    for k in (2, 1, 0):
        hops[k].wait_recv()
        final = final + rrx[k].astype(jnp.float32)
    from_row = lax.broadcasted_iota(jnp.int32, (2 * W, 2 * W), 0)
    to_col = lax.broadcasted_iota(jnp.int32, (2 * W, 2 * W), 1)
    place = (to_col == 2 * lax.rem(from_row, W) + from_row // W).astype(jnp.float32).astype(jnp.bfloat16)
    out_ref[0] = lax.dot_general(
        final.astype(jnp.bfloat16), place, (((0,), (0,)), ((), ())), preferred_element_type=jnp.float32
    )
    for copy in (
        own_y0, own_z1, own_y1, own_z0, own_c, d_z0, y0_c, d_y1, z1_c, y1_c, z0_c, d0_c, d1_c,
        swap, *core, *hops,
    ):
        copy.wait_send()


def fused(frames, conv_tiles, up_tiles):
    shard, _, voxels = frames.shape
    _, taps, depth, filters = conv_tiles.shape
    _, up_taps, outs, _ = up_tiles.shape
    height = voxels // W
    tile = 2 * W
    bf, f32 = jnp.bfloat16, jnp.float32
    dma = pltpu.SemaphoreType.DMA
    operands = (frames.transpose(1, 0, 2), conv_tiles, up_tiles)
    return pl.pallas_call(
        fused_kernel,
        out_shape=jax.ShapeDtypeStruct((1, outs, tile), f32),
        in_specs=[
            pl.BlockSpec(memory_space=pltpu.HBM),
            pl.BlockSpec(memory_space=pltpu.HBM),
            pl.BlockSpec(memory_space=pltpu.HBM),
        ],
        out_specs=pl.BlockSpec(memory_space=pltpu.VMEM),
        scratch_shapes=[
            pltpu.VMEM((3, depth, voxels), bf),
            pltpu.VMEM((taps, depth, filters), bf),
            pltpu.VMEM((up_taps, outs, filters), bf),
            pltpu.VMEM((2, 2, outs, 4 * filters), bf),
            pltpu.VMEM((voxels, 9 * filters), f32),
            pltpu.VMEM((voxels, filters), f32),
            pltpu.VMEM((voxels, filters), bf),
            pltpu.VMEM((voxels, filters), bf),
            pltpu.VMEM((3, voxels + 2 * W, filters), bf),
            pltpu.VMEM((height, tile, outs), f32),
            pltpu.VMEM((height, tile, outs), bf),
            pltpu.VMEM((height, tile, outs), bf),
            pltpu.VMEM((3, tile, outs), bf),
            pltpu.VMEM((3, tile, outs), bf),
            dma((4,)),
            dma((13,)), dma((13,)),
            dma((1,)), dma((1,)),
            dma((4,)), dma((4,)),
            dma((3,)), dma((3,)),
            pltpu.SemaphoreType.REGULAR,
        ],
        compiler_params=pltpu.CompilerParams(
            collective_id=0, has_side_effects=True, vmem_limit_bytes=24 << 20
        ),
    )(*(pltpu.with_memory_space_constraint(x, pltpu.HBM) for x in operands)).astype(bf)


def route(frames, conv_tiles, up_tiles):
    blocks = lax.axis_size("rows") // 8
    tile_rows = frames.shape[2] // W // 4
    if blocks == 2 and tile_rows == 1 and frames.shape[0] * 8 == conv_tiles.shape[2]:
        return fused(frames, conv_tiles, up_tiles)
    return on_device(frames, conv_tiles, up_tiles)


def solution(mesh):
    return jax.shard_map(
        route,
        mesh=mesh,
        in_specs=(
            P(("groups", "rows"), None, None),
            P("rows", None, None, None),
            P("rows", None, None, None),
        ),
        out_specs=P(("groups", "rows"), None, None),
        check_vma=False,
    )
```

```python
import jax
import jax.numpy as jnp
from jax import lax
from jax.experimental import pallas as pl
from jax.experimental.pallas import tpu as pltpu
from jax.sharding import PartitionSpec as P

W = 64


def partner_2(block, axis, stride):
    count = lax.axis_size(axis)
    route = []
    for low in range(count):
        high = low | 1 << stride
        if high != low and high < count:
            route += [(low, high), (high, low)]
    return lax.ppermute(block, axis, route)


def shift_plane(planes, row_step, col_step):
    height = planes.shape[-2]
    width = planes.shape[-1]
    padded = jnp.pad(planes, [(0, 0)] * (planes.ndim - 2) + [(1, 1), (1, 1)])
    return padded[..., 1 + row_step : 1 + row_step + height, 1 + col_step : 1 + col_step + width]


def phase_groups(phase):
    if phase == 0:
        return [(-1, (0,)), (0, (1, 2))]
    return [(0, (0, 1)), (1, (2,))]


def upper_side(device_index, level):
    return device_index >> level & 1 == 1


def collect_channels(pieces, device_index):
    for level in range(3):
        partner = partner_2(pieces, "rows", level)
        pieces = jnp.where(
            upper_side(device_index, level),
            jnp.concatenate([partner, pieces], 0),
            jnp.concatenate([pieces, partner], 0),
        )
    return pieces


def halve_partials(totals, device_index, levels):
    for level in levels:
        middle = totals.shape[1] // 2
        upper_half = upper_side(device_index, level)
        kept_part = jnp.where(upper_half, totals[:, middle:], totals[:, :middle])
        sent_part = jnp.where(upper_half, totals[:, :middle], totals[:, middle:])
        totals = kept_part + partner_2(sent_part, "rows", level)
    return totals


def halve_outputs(totals, device_index):
    for level in (2, 1, 0):
        middle = totals.shape[1] // 2
        upper_half = upper_side(device_index, level)
        kept_part = jnp.where(upper_half, totals[:, middle:], totals[:, :middle])
        sent_part = jnp.where(upper_half, totals[:, :middle], totals[:, middle:])
        totals = kept_part + partner_2(sent_part.astype(jnp.bfloat16), "rows", level).astype(
            sent_part.dtype
        )
    return totals


def on_device(frames, conv_tiles, up_tiles):
    device_index = lax.axis_index("rows")
    bit_count = lax.axis_size("rows").bit_length() - 1
    pieces = collect_channels(frames, device_index)
    in_channels = pieces.shape[0]
    voxels = pieces.shape[2]
    height = voxels // W
    volume = pieces.reshape(in_channels, 3, height, W)
    filters = conv_tiles.shape[3]
    partial_value = jnp.zeros((filters, voxels), jnp.float32)
    for time_tap in range(3):
        planes = []
        for spatial_tap in range(9):
            row_tap = spatial_tap // 3
            col_tap = spatial_tap % 3
            planes.append(
                shift_plane(volume[:, time_tap], row_tap - 1, col_tap - 1).reshape(
                    in_channels, voxels
                )
            )
        columns = jnp.concatenate(planes, 0)
        weights = conv_tiles[0, 9 * time_tap : 9 * time_tap + 9].reshape(9 * in_channels, filters)
        partial_value = partial_value + lax.dot_general(
            weights, columns, (((0,), (0,)), ((), ())), preferred_element_type=jnp.float32
        )
    summed = halve_partials(partial_value, device_index, list(range(bit_count - 1, 2, -1)))
    hidden_block = jax.nn.silu(summed).astype(jnp.bfloat16)
    for level in range(3, bit_count):
        partner = partner_2(hidden_block, "rows", level)
        hidden_block = jnp.where(
            upper_side(device_index, level),
            jnp.concatenate([partner, hidden_block], 1),
            jnp.concatenate([hidden_block, partner], 1),
        )
    hidden_planes = hidden_block.reshape(filters, height, W)
    up_weight = up_tiles[0].astype(jnp.float32)
    out_channels = up_weight.shape[1]
    phase_rows = []
    for row_phase in range(2):
        phase_cols = []
        for col_phase in range(2):
            weight_parts = []
            plane_parts = []
            for row_shift, row_taps in phase_groups(row_phase):
                for col_shift, col_taps in phase_groups(col_phase):
                    combined = jnp.zeros((out_channels, filters), jnp.float32)
                    for row_tap in row_taps:
                        for col_tap in col_taps:
                            combined = combined + up_weight[3 * row_tap + col_tap]
                    weight_parts.append(combined.astype(jnp.bfloat16))
                    plane_parts.append(
                        shift_plane(hidden_planes, row_shift, col_shift).reshape(filters, voxels)
                    )
            stacked_weight = jnp.concatenate(weight_parts, 1)
            stacked_planes = jnp.concatenate(plane_parts, 0)
            phase_out = jnp.dot(stacked_weight, stacked_planes, preferred_element_type=jnp.float32)
            phase_cols.append(phase_out.reshape(out_channels, height, W))
        phase_rows.append(jnp.stack(phase_cols, 0))
    phased = jnp.stack(phase_rows, 0)
    result = phased.transpose(2, 3, 0, 4, 1).reshape(out_channels, 4 * voxels)
    summed_out = halve_outputs(result, device_index)
    return summed_out.astype(jnp.bfloat16).reshape(1, out_channels, summed_out.shape[1])


MESH = pl.DeviceIdType.MESH


def fused_kernel(
    frames_ref, conv_hbm, up_hbm, out_ref,
    xg, wbuf, upbuf, pw, zacc, partial, pbuf, prx, hp, ownp, sbuf, crx, rbuf, rrx,
    lsem, gs, gr, ps, pr, cs_, cr, rs, rr, ready,
):
    me = lax.axis_index("rows")
    f = lax.rem(me, 8)
    half = me // 8
    c = lax.rem(f, 2)
    y = lax.rem(f // 2, 2)
    z = f // 4
    dc, dy, dz = 1 - 2 * c, 2 - 4 * y, 4 - 8 * z
    pc, py, pz, pd = me + dc, me + dy, me + dz, me + dy + dz
    far = me + 8 - 16 * half
    _, shard, voxels = frames_ref.shape
    height = voxels // W
    depth = wbuf.shape[1] // 2
    filters = wbuf.shape[2]
    piece = shard // 2

    def weight_copy(k, which):
        rows = pl.ds(pl.multiple_of(which * depth, depth), depth)
        return pltpu.make_async_copy(conv_hbm.at[0, :, rows, :], wbuf.at[:, rows, :], lsem.at[k])

    w_near = weight_copy(0, z)
    w_far = weight_copy(1, 1 - z)
    up_copy = pltpu.make_async_copy(up_hbm.at[0], upbuf, lsem.at[2])

    own_copy = pltpu.make_async_copy(
        frames_ref, xg.at[:, pl.ds(pl.multiple_of(f * shard, shard), shard), :], lsem.at[3]
    )
    barrier = pltpu.get_barrier_semaphore()
    for peer in (pc, py, pz):
        pl.semaphore_signal(barrier, inc=1, device_id={"rows": peer}, device_id_type=MESH)
    inner_chip = lax.rem(z + half, 2)
    middle = inner_chip == 1
    across = me + 4 - 8 * half

    @pl.when(middle)
    def _():
        pl.semaphore_signal(barrier, inc=1, device_id={"rows": across}, device_id_type=MESH)

    own_copy.start()
    w_near.start()
    up_copy.start()
    w_far.start()
    pl.semaphore_wait(barrier, 3 + inner_chip)

    @pl.when(middle)
    def _():
        pl.semaphore_signal(ready, inc=1, device_id={"rows": across}, device_id_type=MESH)

    own_copy.wait()

    def send(src, dst, ssem, rsem, k, peer):
        return pltpu.make_async_remote_copy(
            src_ref=src, dst_ref=dst, send_sem=ssem.at[k], recv_sem=rsem.at[k],
            device_id={"rows": peer}, device_id_type=MESH,
        )

    def gather(k, slot, part, peer):
        if part is None:
            view = xg.at[:, pl.ds(pl.multiple_of(slot * shard, shard), shard), :]
        else:
            view = xg.at[:, pl.ds(pl.multiple_of(slot * shard + part * piece, piece), piece), :]
        return send(view, view, gs, gr, k, peer)

    sy, sz, sd = f + dy, f + dz, f + dy + dz
    own_y0 = gather(0, f, 0, py)
    own_z1 = gather(1, f, 1, pz)
    own_y1 = gather(2, f, 1, py)
    own_z0 = gather(3, f, 0, pz)
    own_c = gather(4, f, None, pc)
    for copy in (own_y0, own_z1, own_c, own_y1, own_z0):
        copy.start()

    edge = jnp.zeros((W, filters), jnp.bfloat16)
    for s in range(3):
        hp[s, :W, :] = edge
        hp[s, W + voxels :, :] = edge
    up_copy.wait()
    for p in range(2):
        for q in range(2):
            for k, (_, row_taps) in enumerate(phase_groups(p)):
                for l, (_, col_taps) in enumerate(phase_groups(q)):
                    total = None
                    for b in row_taps:
                        for e in col_taps:
                            tap = upbuf[3 * b + e].astype(jnp.float32)
                            total = tap if total is None else total + tap
                    at = (2 * k + l) * filters
                    pw[p, q, :, at : at + filters] = total.astype(jnp.bfloat16)

    own_y0.wait_recv()
    d_z0 = gather(5, sy, 0, pz)
    d_z0.start()
    y0_c = gather(6, sy, 0, pc)
    y0_c.start()
    own_z1.wait_recv()
    d_y1 = gather(7, sz, 1, py)
    d_y1.start()
    z1_c = gather(8, sz, 1, pc)
    z1_c.start()
    own_y1.wait_recv()
    y1_c = gather(9, sy, 1, pc)
    y1_c.start()
    own_z0.wait_recv()
    z0_c = gather(10, sz, 0, pc)
    z0_c.start()

    def conv_half(which, first):
        rows = pl.ds(pl.multiple_of(which * depth, depth), depth)
        xt = jnp.concatenate([xg[a, rows, :].T for a in range(3)], axis=1)
        for t in range(0, 9, 2):
            taps = [t, t + 1] if t + 1 < 9 else [t]
            rhs = jnp.concatenate(
                [jnp.concatenate([wbuf[9 * a + tap, rows, :] for a in range(3)], 0) for tap in taps], 1
            )
            got = jnp.dot(xt, rhs, preferred_element_type=jnp.float32)
            lanes = slice(t * filters, (t + len(taps)) * filters)
            if first:
                zacc[:, lanes] = got
            else:
                zacc[:, lanes] = zacc[:, lanes] + got

    own_c.wait_recv()
    y0_c.wait_recv()
    y1_c.wait_recv()
    w_near.wait()
    conv_half(z, True)

    d_z0.wait_recv()
    d0_c = gather(11, sd, 0, pc)
    d0_c.start()
    d_y1.wait_recv()
    d1_c = gather(12, sd, 1, pc)
    d1_c.start()
    z0_c.wait_recv()
    z1_c.wait_recv()
    w_far.wait()
    d0_c.wait_recv()
    d1_c.wait_recv()
    conv_half(1 - z, False)

    column = lax.rem(lax.broadcasted_iota(jnp.int32, (voxels, filters), 0), W)
    at_left = column == 0
    at_right = column == W - 1
    blank = jnp.zeros((W, filters), jnp.float32)
    sums = []
    for e in range(3):
        up_tap, mid_tap, low_tap = (
            zacc[:, (3 * b + e) * filters : (3 * b + e + 1) * filters] for b in range(3)
        )
        sums.append(
            mid_tap
            + jnp.concatenate([blank, up_tap[: voxels - W]], 0)
            + jnp.concatenate([low_tap[W:], blank], 0)
        )
    total = (
        sums[1]
        + jnp.where(at_left, 0.0, pltpu.roll(sums[0], 1, 0))
        + jnp.where(at_right, 0.0, pltpu.roll(sums[2], voxels - 1, 0))
    )
    pbuf[...] = total.astype(jnp.bfloat16)
    swap = send(pbuf, prx, ps, pr, 0, far)

    @pl.when(middle)
    def _():
        pl.semaphore_wait(ready, 1)

    swap.start()
    partial[...] = total
    swap.wait_recv()
    pre = partial[...] + prx[...].astype(jnp.float32)
    hidden = (pre / (1.0 + jnp.exp(-pre))).astype(jnp.bfloat16).astype(jnp.float32)
    inner = slice(W, W + voxels)
    hp[0, inner, :] = jnp.where(at_left, 0.0, pltpu.roll(hidden, 1, 0)).astype(jnp.bfloat16)
    hp[1, inner, :] = hidden.astype(jnp.bfloat16)
    hp[2, inner, :] = jnp.where(at_right, 0.0, pltpu.roll(hidden, voxels - 1, 0)).astype(jnp.bfloat16)

    def phase(p, target):
        for q in range(2):
            planes = jnp.concatenate(
                [
                    hp[q + l, pl.ds(pl.multiple_of((p + k) * W, W), voxels), :]
                    for k in range(2)
                    for l in range(2)
                ],
                1,
            )
            got = lax.dot_general(
                planes, pw[p, q], (((1,), (1,)), ((), ())), preferred_element_type=jnp.float32
            ).astype(target.dtype)
            for row in range(height):
                target[row, q * W : (q + 1) * W, :] = got[row * W : (row + 1) * W]

    here = 2 * z + y
    to_y = 2 * z + 1 - y
    to_z = 2 * (1 - z) + y
    to_d = 2 * (1 - z) + 1 - y
    phase(1 - c, sbuf)
    core = [send(sbuf.at[row], crx.at[row], cs_, cr, k, pc) for k, row in enumerate((to_d, to_z, to_y, here))]
    for copy in core:
        copy.start()
    phase(c, ownp)
    from_row = lax.broadcasted_iota(jnp.int32, (2 * W, 2 * W), 0)
    to_col = lax.broadcasted_iota(jnp.int32, (2 * W, 2 * W), 1)
    place = (to_col == 2 * lax.rem(from_row, W) + from_row // W).astype(jnp.float32).astype(jnp.bfloat16)
    hops = []
    for k, (row, peer) in enumerate(((to_d, pd), (to_z, pz), (to_y, py))):
        core[k].wait_recv()
        rbuf[k] = (ownp[row] + crx[row].astype(jnp.float32)).astype(jnp.bfloat16)
        hop = send(rbuf.at[k], rrx.at[k], rs, rr, k, peer)
        hop.start()
        hops.append(hop)
    core[3].wait_recv()
    final = ownp[here] + crx[here].astype(jnp.float32)
    for k in (2, 1, 0):
        hops[k].wait_recv()
        final = final + rrx[k].astype(jnp.float32)
    out_ref[0] = lax.dot_general(
        final.astype(jnp.bfloat16), place, (((0,), (0,)), ((), ())), preferred_element_type=jnp.float32
    )
    for copy in (
        own_y0, own_z1, own_y1, own_z0, own_c, d_z0, y0_c, d_y1, z1_c, y1_c, z0_c, d0_c, d1_c,
        swap, *core, *hops,
    ):
        copy.wait_send()


def fused(frames, conv_tiles, up_tiles):
    shard, _, voxels = frames.shape
    _, taps, depth, filters = conv_tiles.shape
    _, up_taps, outs, _ = up_tiles.shape
    height = voxels // W
    tile = 2 * W
    bf, f32 = jnp.bfloat16, jnp.float32
    dma = pltpu.SemaphoreType.DMA
    operands = (frames.transpose(1, 0, 2), conv_tiles, up_tiles)
    return pl.pallas_call(
        fused_kernel,
        out_shape=jax.ShapeDtypeStruct((1, outs, tile), f32),
        in_specs=[
            pl.BlockSpec(memory_space=pltpu.HBM),
            pl.BlockSpec(memory_space=pltpu.HBM),
            pl.BlockSpec(memory_space=pltpu.HBM),
        ],
        out_specs=pl.BlockSpec(memory_space=pltpu.VMEM),
        scratch_shapes=[
            pltpu.VMEM((3, depth, voxels), bf),
            pltpu.VMEM((taps, depth, filters), bf),
            pltpu.VMEM((up_taps, outs, filters), bf),
            pltpu.VMEM((2, 2, outs, 4 * filters), bf),
            pltpu.VMEM((voxels, 9 * filters), f32),
            pltpu.VMEM((voxels, filters), f32),
            pltpu.VMEM((voxels, filters), bf),
            pltpu.VMEM((voxels, filters), bf),
            pltpu.VMEM((3, voxels + 2 * W, filters), bf),
            pltpu.VMEM((height, tile, outs), f32),
            pltpu.VMEM((height, tile, outs), bf),
            pltpu.VMEM((height, tile, outs), bf),
            pltpu.VMEM((3, tile, outs), bf),
            pltpu.VMEM((3, tile, outs), bf),
            dma((4,)),
            dma((13,)), dma((13,)),
            dma((1,)), dma((1,)),
            dma((4,)), dma((4,)),
            dma((3,)), dma((3,)),
            pltpu.SemaphoreType.REGULAR,
        ],
        compiler_params=pltpu.CompilerParams(
            collective_id=0, has_side_effects=True, vmem_limit_bytes=24 << 20
        ),
    )(*(pltpu.with_memory_space_constraint(x, pltpu.HBM) for x in operands)).astype(bf)


def route(frames, conv_tiles, up_tiles):
    blocks = lax.axis_size("rows") // 8
    tile_rows = frames.shape[2] // W // 4
    if blocks == 2 and tile_rows == 1 and frames.shape[0] * 8 == conv_tiles.shape[2]:
        return fused(frames, conv_tiles, up_tiles)
    return on_device(frames, conv_tiles, up_tiles)


def solution(mesh):
    return jax.shard_map(
        route,
        mesh=mesh,
        in_specs=(
            P(("groups", "rows"), None, None),
            P("rows", None, None, None),
            P("rows", None, None, None),
        ),
        out_specs=P(("groups", "rows"), None, None),
        check_vma=False,
    )
```
